32 devices in a mesh: section: 4 (over y, x), row: 2 (over core), col: 4 (over z).
Axes of the slice: x: 2, y: 2, z: 4, core: 2. Of those that a mesh axis runs over, the one named last changes fastest.
Arguments:
- cotangent: float32 [4, 128, 4096], P('section', None, ('row', 'col')), may hold values from -6 to 6
- incoming: float32 [4, 128, 4096], P('section', None, ('row', 'col')), may hold values from -6 to 6
- upd_u: float32 [4, 8, 128, 4096], P('section', None, None, ('row', 'col')), may hold values from -4 to 4
- upd_v: float32 [4, 8, 128, 4096], P('section', None, None, ('row', 'col')), may hold values from -0.0078125 to 0.0078125
- saved_x: bfloat16 [4, 4, 128, 4096], P('section', None, None, ('row', 'col')), may hold values from -6 to 6
- saved_h: bfloat16 [4, 4, 2, 128, 14336], P('section', None, None, None, 'col'), may hold values from -6 to 6
- norm_gain: float32 [4, 4096], P('section', ('row', 'col')), may hold values from 0.25 to 1.75
- w_gate: bfloat16 [4, 4096, 14336], P('section', 'row', 'col'), may hold values from -0.09375 to 0.09375
- w_up: bfloat16 [4, 4096, 14336], P('section', 'row', 'col'), may hold values from -0.09375 to 0.09375
- w_down: bfloat16 [4, 14336, 4096], P('section', 'col', 'row'), may hold values from -0.046875 to 0.046875
Outputs:
- new_cotangent: float32 [4, 128, 4096], P('section', None, ('row', 'col'))
- residual_out: float32 [4, 128, 4096], P('section', None, ('row', 'col'))
The draws below stay inside these ranges and needn't reach their ends.
All inputs are finite; a program needn't handle non-finite values.
Results may differ from the reference program's by a relative error of at most 0.014.
Values may be sent and summed in bfloat16 or wider, within the bound.
No kernel may reach another device: no remote copies, remote signals or barrier semaphores. Data moves between devices by JAX's collectives and lax.ppermute only.
A program may use at most 128 MiB of HBM per device.

```python
import jax
import jax.numpy as jnp
from jax import lax

D = 4096
FF = 14336
ROWS = 128
UPD = 8
LAYERS = 4
MB = 4


def shard_levels(stream_key, shape, cuts, least, top_value):
    def one(axis_at, blocks):
        draws = jax.random.uniform(jax.random.fold_in(jax.random.fold_in(stream_key, 6), axis_at), (blocks,), jnp.float32, least / len(cuts), top_value / len(cuts))
        return jnp.repeat(jnp.exp(draws), shape[axis_at] // blocks).reshape((-1,) + (1,) * (len(shape) - axis_at - 1))

    level = one(*cuts[0])
    for cut in cuts[1:]:
        level = level * one(*cut)
    return level


def noise(rng, extent, deviation, reach, split=(), kind=jnp.bfloat16):
    array = jax.random.normal(rng, extent, jnp.float32) * deviation
    if len(split) > 0:
        array = shard_levels(rng, extent, split, -0.22, 0.18) * array
    return jnp.clip(array, min=-reach, max=reach).astype(kind)


def setup_inputs(seed: int = 0) -> dict:
    streams_of = jax.random.split(jax.random.key(seed), 11)
    return {
        "cotangent": noise(streams_of[0], (MB, ROWS, D), 1.0, 6.0, ((0, 4), (2, 8)), jnp.float32),
        "incoming": noise(streams_of[1], (MB, ROWS, D), 1.0, 6.0, ((0, 4), (2, 8)), jnp.float32),
        "upd_u": noise(streams_of[2], (MB, UPD, ROWS, D), 0.3, 4.0, ((0, 4), (3, 8)), jnp.float32),
        "upd_v": noise(streams_of[3], (MB, UPD, ROWS, D), (ROWS * D) ** -0.5, 0.0078125, ((0, 4), (3, 8)), jnp.float32),
        "saved_x": noise(streams_of[4], (LAYERS, MB, ROWS, D), 1.0, 6.0, ((0, 4), (3, 8))),
        "saved_h": noise(streams_of[5], (LAYERS, MB, 2, ROWS, FF), 1.5, 6.0, ((0, 4), (4, 4))),
        "norm_gain": jnp.clip(1.0 + 0.15 * jax.random.normal(streams_of[6], (LAYERS, D), jnp.float32), 0.25, 1.75),
        "w_gate": noise(streams_of[7], (LAYERS, D, FF), D ** -0.5, 0.09375, ((0, 4), (1, 2), (2, 4))),
        "w_up": noise(streams_of[8], (LAYERS, D, FF), D ** -0.5, 0.09375, ((0, 4), (1, 2), (2, 4))),
        "w_down": noise(streams_of[9], (LAYERS, FF, D), FF ** -0.5, 0.046875, ((0, 4), (1, 4), (2, 2))),
    }


eps = 1e-05

def layer_back(c, x, hpair, gain, wg, wu, wd):
    gy = c.astype(jnp.bfloat16)
    ga = jnp.dot(gy, wd.T, preferred_element_type=jnp.float32)
    hg = hpair[0].astype(jnp.float32)
    hu = hpair[1].astype(jnp.float32)
    sig = jax.nn.sigmoid(hg)
    grad_gate = (ga * hu * sig * (1.0 + hg * (1.0 - sig))).astype(jnp.bfloat16)
    grad_up = (ga * hg * sig).astype(jnp.bfloat16)
    normgrad = jnp.dot(grad_gate, wg.T, preferred_element_type=jnp.float32) + jnp.dot(grad_up, wu.T, preferred_element_type=jnp.float32)
    xf = x.astype(jnp.float32)
    rstd = lax.rsqrt(lax.optimization_barrier(jnp.sum(xf * xf, axis=-1, keepdims=True)) / D + eps)
    scaled = gain * normgrad
    inner = lax.optimization_barrier(jnp.sum(scaled * xf, axis=-1, keepdims=True)) / D
    return c + rstd * scaled - xf * (rstd * rstd * rstd) * inner

def reference(cotangent, incoming, upd_u, upd_v, saved_x, saved_h, norm_gain, w_gate, w_up, w_down):
    new_list = []
    res_list = []
    for micro in range(MB):
        carry = cotangent[micro]
        for layer in range(LAYERS - 1, -1, -1):
            carry = layer_back(carry, saved_x[layer, micro], saved_h[layer, micro], norm_gain[layer], w_gate[layer], w_up[layer], w_down[layer])
        resid = carry + incoming[micro] - cotangent[micro]
        dots = jnp.einsum('urd,rd->u', upd_v[micro], resid, precision=lax.Precision.HIGHEST)
        update = jnp.einsum('u,urd->rd', dots, upd_u[micro], precision=lax.Precision.HIGHEST)
        new_list.append(cotangent[micro] + resid - update)
        res_list.append(resid)
    return (jnp.stack(new_list), jnp.stack(res_list))
```

```python
import functools

import jax
import jax.numpy as jnp
from jax import lax
from jax.experimental import pallas as pl
from jax.experimental.pallas import tpu as pltpu
from jax.sharding import PartitionSpec as P

D = 4096


eps = 1e-05

NT = (((1,), (1,)), ((), ()))
VMEM = pl.BlockSpec(memory_space=pltpu.VMEM)
ANY = pl.BlockSpec(memory_space=pl.ANY)


def shifted(x, axis, by):
    devices = lax.axis_size(axis)
    return lax.ppermute(x, axis, [(i, (i + by) % devices) for i in range(devices)])


def rotate(carry):
    return shifted(carry, "section", -1)


def spread(x, by):
    sections, cols = lax.axis_size("section"), lax.axis_size("col")
    pairs = [
        (s * cols + c, ((s - 1) % sections) * cols + (c + by) % cols)
        for s in range(sections)
        for c in range(cols)
    ]
    return lax.ppermute(x, ("section", "col"), pairs)


def group_sum(x):
    rows, cols = lax.axis_size("row"), lax.axis_size("col")
    total = x
    for r in range(rows):
        for c in range(cols):
            if r == 0 and c == 0:
                continue
            pairs = [
                (i * cols + j, ((i + r) % rows) * cols + (j + c) % cols)
                for i in range(rows)
                for j in range(cols)
            ]
            total = total + lax.ppermute(x, ("row", "col"), pairs)
    return total


def down_kernel(cols, depth, tile, *refs):
    pieces, w_ref, o_ref = refs[:cols], refs[cols], refs[cols + 1]
    buf, gy, sem = refs[cols + 2 :]
    tiles = w_ref.shape[0] // tile
    chunk = gy.shape[1] // cols

    def fetch(i):
        return pltpu.make_async_copy(
            w_ref.at[pl.ds(i * tile, tile)], buf.at[i % depth], sem.at[i % depth]
        )

    for i in range(min(depth, tiles)):
        fetch(i).start()
    col = lax.axis_index("col")
    for j in range(cols):
        source = lax.rem(col + cols - j, cols)
        gy[:, pl.ds(pl.multiple_of(source * chunk, chunk), chunk)] = pieces[j][...]
    for i in range(tiles):
        fetch(i).wait()
        o_ref[:, i * tile : (i + 1) * tile] = lax.dot_general(
            gy[...], buf[i % depth], NT, preferred_element_type=jnp.float32
        ).astype(o_ref.dtype)
        if i + depth < tiles:
            fetch(i + depth).start()


def down(pieces, wd):
    cols = len(pieces)
    rows = pieces[0].shape[0]
    width, feats = wd.shape
    tile, depth = 512, 5
    return pl.pallas_call(
        functools.partial(down_kernel, cols, depth, tile),
        in_specs=[VMEM] * cols + [ANY],
        out_specs=VMEM,
        out_shape=jax.ShapeDtypeStruct((rows, width), jnp.bfloat16),
        scratch_shapes=[
            pltpu.VMEM((depth, tile, feats), wd.dtype),
            pltpu.VMEM((rows, feats), jnp.bfloat16),
            pltpu.SemaphoreType.DMA((depth,)),
        ],
        compiler_params=pltpu.CompilerParams(vmem_limit_bytes=24 << 20),
        cost_estimate=pl.CostEstimate(
            flops=2 * rows * width * feats, bytes_accessed=2 * width * feats, transcendentals=0
        ),
    )(*pieces, wd)


def up_kernel(step, cols, depth, tile, ga_ref, gb_ref, h_ref, wg_ref, wu_ref, *refs):
    outs = refs[:cols]
    hbuf, gate, upper, gbuf, ubuf, hsem, sem = refs[cols:]
    feats, width = wg_ref.shape
    chunk = feats // cols
    parts = chunk // tile
    sections = h_ref.shape[1]
    micro = lax.rem(lax.axis_index("section") + step + 1, sections)
    col = lax.axis_index("col")
    order = [(j, p) for j in list(range(1, cols)) + [0] for p in range(parts)]

    def fetch(i):
        j, p = order[i]
        dest = lax.rem(col + j, cols)
        first = pl.multiple_of(dest * chunk + p * tile, tile)
        s = i % depth
        return (
            pltpu.make_async_copy(wg_ref.at[pl.ds(first, tile)], gbuf.at[s], sem.at[0, s]),
            pltpu.make_async_copy(wu_ref.at[pl.ds(first, tile)], ubuf.at[s], sem.at[1, s]),
        )

    hcopy = pltpu.make_async_copy(h_ref.at[0, micro], hbuf, hsem.at[0])
    hcopy.start()
    for i in range(min(depth, len(order))):
        for c in fetch(i):
            c.start()
    hcopy.wait()
    block = 512
    for b in range(width // block):
        at = slice(b * block, (b + 1) * block)
        ga = ga_ref[:, at].astype(jnp.float32) + gb_ref[:, at].astype(jnp.float32)
        hg = hbuf[0, :, at].astype(jnp.float32)
        hu = hbuf[1, :, at].astype(jnp.float32)
        sig = jax.nn.sigmoid(hg)
        gate[:, at] = (ga * hu * sig * (1.0 + hg * (1.0 - sig))).astype(jnp.bfloat16)
        upper[:, at] = (ga * hg * sig).astype(jnp.bfloat16)
    for i, (j, p) in enumerate(order):
        for c in fetch(i):
            c.wait()
        s = i % depth
        acc = lax.dot_general(gate[...], gbuf[s], NT, preferred_element_type=jnp.float32)
        acc += lax.dot_general(upper[...], ubuf[s], NT, preferred_element_type=jnp.float32)
        outs[j][:, p * tile : (p + 1) * tile] = acc.astype(outs[j].dtype)
        if i + depth < len(order):
            for c in fetch(i + depth):
                c.start()


def up(step, ga, gb, hidden, wg, wu, cols):
    rows = ga.shape[0]
    feats, width = wg.shape
    chunk = feats // cols
    tile, depth = 256, 4
    return pl.pallas_call(
        functools.partial(up_kernel, step, cols, depth, tile),
        in_specs=[VMEM, VMEM, ANY, ANY, ANY],
        out_specs=[VMEM] * cols,
        out_shape=[
            jax.ShapeDtypeStruct((rows, chunk), jnp.float32 if j == 0 else jnp.bfloat16)
            for j in range(cols)
        ],
        scratch_shapes=[
            pltpu.VMEM((2, rows, width), hidden.dtype),
            pltpu.VMEM((rows, width), jnp.bfloat16),
            pltpu.VMEM((rows, width), jnp.bfloat16),
            pltpu.VMEM((depth, tile, width), wg.dtype),
            pltpu.VMEM((depth, tile, width), wu.dtype),
            pltpu.SemaphoreType.DMA((1,)),
            pltpu.SemaphoreType.DMA((2, depth)),
        ],
        compiler_params=pltpu.CompilerParams(vmem_limit_bytes=40 << 20),
        cost_estimate=pl.CostEstimate(
            flops=4 * rows * width * feats, bytes_accessed=4 * width * feats, transcendentals=0
        ),
    )(ga, gb, hidden, wg, wu)


def shards(cotangent, incoming, upd_u, upd_v, saved_x, saved_h, norm_gain, w_gate, w_up, w_down):
    sections, cols = lax.axis_size("section"), lax.axis_size("col")
    section_idx = lax.axis_index("section")
    inputs_all = saved_x[0].astype(jnp.float32)
    gain = norm_gain[0]
    wg, wu, wd = w_gate[0], w_up[0], w_down[0]
    sumsq_all = group_sum(jnp.sum(inputs_all * inputs_all, axis=2))
    rstd_all = lax.rsqrt(sumsq_all / D + eps)

    carry = cotangent[0]
    for step in range(2 * sections - 1):
        gy = carry.astype(jnp.bfloat16)
        pieces = [spread(gy, j) for j in range(cols)]
        carry = rotate(carry)
        micro = (section_idx + step + 1) % sections
        ga = down(pieces, wd)
        gb = shifted(ga, "row", 1)
        outs = up(step, ga, gb, saved_h, wg, wu, cols)
        normgrad = outs[0]
        for j in range(1, cols):
            normgrad = normgrad + shifted(outs[j], "col", j).astype(jnp.float32)
        xf = lax.dynamic_index_in_dim(inputs_all, micro, 0, keepdims=False)
        rstd = lax.dynamic_index_in_dim(rstd_all, micro, 0, keepdims=False)[:, None]
        scaled = gain * normgrad
        inner = group_sum(jnp.sum(scaled * xf, axis=1))[:, None] / D
        updated = carry + rstd * scaled - xf * (rstd * rstd * rstd) * inner
        active = jnp.logical_and(step >= micro, step - micro < sections)
        carry = jnp.where(active, updated, carry)

    pulled = rotate(carry)
    resid = pulled + incoming[0] - cotangent[0]
    local_dots = jnp.einsum("urd,rd->u", upd_v[0], resid, precision=lax.Precision.HIGHEST)
    dots = group_sum(local_dots)
    update = jnp.einsum("u,urd->rd", dots, upd_u[0], precision=lax.Precision.HIGHEST)
    fresh = cotangent[0] + resid - update
    return (fresh[None], resid[None])


def plain_shards(cotangent, incoming, upd_u, upd_v, saved_x, saved_h, norm_gain, w_gate, w_up, w_down):
    sections = lax.axis_size("section")
    section_idx = lax.axis_index("section")
    inputs_all = saved_x[0].astype(jnp.float32)
    hidden_all = saved_h[0]
    gain = norm_gain[0]
    wg = w_gate[0]
    wu = w_up[0]
    wd = w_down[0]

    def layer_step(step, carry):
        carry = rotate(carry)
        micro = (section_idx + step + 1) % sections
        xf = lax.dynamic_index_in_dim(inputs_all, micro, 0, keepdims=False)
        hpair = lax.dynamic_index_in_dim(hidden_all, micro, 0, keepdims=False)
        sumsq = lax.psum(jnp.sum(xf * xf, axis=1), ("row", "col"))
        gy = carry.astype(jnp.bfloat16)
        wide = lax.all_gather(gy, "col", axis=1, tiled=True)
        ga_part = lax.dot_general(wide, wd, NT, preferred_element_type=jnp.float32)
        ga = lax.psum_scatter(ga_part, "row", scatter_dimension=1, tiled=True)
        width = ga.shape[1]
        offset = lax.axis_index("row") * width
        hg = lax.dynamic_slice_in_dim(hpair[0], offset, width, 1).astype(jnp.float32)
        hu = lax.dynamic_slice_in_dim(hpair[1], offset, width, 1).astype(jnp.float32)
        sig = jax.nn.sigmoid(hg)
        part_gate = (ga * hu * sig * (1.0 + hg * (1.0 - sig))).astype(jnp.bfloat16)
        part_up = (ga * hg * sig).astype(jnp.bfloat16)
        grad_gate = lax.all_gather(part_gate, "row", axis=1, tiled=True)
        grad_up = lax.all_gather(part_up, "row", axis=1, tiled=True)
        first = lax.dot_general(wg, grad_gate, NT, preferred_element_type=jnp.float32)
        second = lax.dot_general(wu, grad_up, NT, preferred_element_type=jnp.float32)
        normgrad = lax.psum_scatter(first + second, "col", scatter_dimension=0, tiled=True).T
        rstd = lax.rsqrt(sumsq / D + eps)[:, None]
        scaled = gain * normgrad
        inner = lax.psum(jnp.sum(scaled * xf, axis=1), ("row", "col"))[:, None] / D
        updated = carry + rstd * scaled - xf * (rstd * rstd * rstd) * inner
        active = jnp.logical_and(step >= micro, step - micro < sections)
        return jnp.where(active, updated, carry)

    pulled = lax.fori_loop(0, 2 * sections - 1, layer_step, cotangent[0])
    pulled = rotate(pulled)
    resid = pulled + incoming[0] - cotangent[0]
    local_dots = jnp.einsum("urd,rd->u", upd_v[0], resid, precision=lax.Precision.HIGHEST)
    dots = lax.psum(local_dots, ("row", "col"))
    update = jnp.einsum("u,urd->rd", dots, upd_u[0], precision=lax.Precision.HIGHEST)
    fresh = cotangent[0] + resid - update
    return (fresh[None], resid[None])


def solution(mesh):
    placed = (
        P("section", None, ("row", "col")),
        P("section", None, ("row", "col")),
        P("section", None, None, ("row", "col")),
        P("section", None, None, ("row", "col")),
        P("section", None, None, ("row", "col")),
        P("section", None, None, None, "col"),
        P("section", ("row", "col")),
        P("section", "row", "col"),
        P("section", "row", "col"),
        P("section", "col", "row"),
    )

    def body(*args):
        chunk, width = args[0].shape[2], args[7].shape[2]
        if lax.axis_size("row") == 2 and chunk % 256 == 0 and width % 512 == 0:
            return shards(*args)
        return plain_shards(*args)

    return jax.shard_map(
        body,
        mesh=mesh,
        in_specs=placed,
        out_specs=(P("section", None, ("row", "col")), P("section", None, ("row", "col"))),
        check_vma=False,
    )
```

```python
import functools

import jax
import jax.numpy as jnp
from jax import lax
from jax.experimental import pallas as pl
from jax.experimental.pallas import tpu as pltpu
from jax.sharding import PartitionSpec as P


D = 4096


eps = 1e-05

NT = (((1,), (1,)), ((), ()))
VMEM = pl.BlockSpec(memory_space=pltpu.VMEM)
HBM = pl.BlockSpec(memory_space=pltpu.HBM)


def in_hbm(x):
    return pltpu.with_memory_space_constraint(x, pltpu.HBM)


def shifted(x, axis, by):
    devices = lax.axis_size(axis)
    return lax.ppermute(x, axis, [(i, (i + by) % devices) for i in range(devices)])


def rotate(carry):
    return shifted(carry, "section", -1)


def swapped(x, axis, by):
    return lax.ppermute(x, axis, [(i, i ^ by) for i in range(lax.axis_size(axis))])


def spread(x, by):
    sections, cols = lax.axis_size("section"), lax.axis_size("col")
    pairs = [
        (s * cols + c, ((s - 1) % sections) * cols + (c ^ by))
        for s in range(sections)
        for c in range(cols)
    ]
    return lax.ppermute(x, ("section", "col"), pairs)


def group_sum(x):
    for axis in ("row", "col"):
        by = 1
        while by < lax.axis_size(axis):
            x = x + swapped(x, axis, by)
            by *= 2
    return x


def micro_of(step, sections):
    return lax.rem(lax.axis_index("section") + step + 1, sections)


def down_kernel(step, side, tile, half, *refs):
    pieces, rest = refs[:half], refs[half:]
    before, rest = (rest[0], rest[1:]) if side else (None, rest)
    w_ref, h_ref, o_ref = rest[:3]
    hout, rest = (None, rest[3:]) if side else (rest[3], rest[4:])
    buf, gy, hsem, sem = rest
    tiles = w_ref.shape[0] // tile
    depth, _, span = buf.shape
    chunk = span // half
    col = lax.axis_index("col")
    group = lax.bitwise_xor(lax.div(col, half), side)
    columns = pl.ds(pl.multiple_of(group * span, span), span)

    def fetch(i):
        s = lax.rem(i, depth)
        first = pl.multiple_of(i * tile, tile)
        return pltpu.make_async_copy(w_ref.at[pl.ds(first, tile), columns], buf.at[s], sem.at[s])

    for i in range(depth - 1):
        fetch(i).start()
    for j in range(half):
        source = lax.bitwise_xor(lax.rem(col, half), j)
        gy[:, pl.ds(pl.multiple_of(source * chunk, chunk), chunk)] = pieces[j][...]
    if not side:
        hcopy = pltpu.make_async_copy(h_ref.at[0, micro_of(step, h_ref.shape[1])], hout, hsem.at[0])

    @pl.loop(0, tiles)
    def _(i):
        fetch(i).wait()

        @pl.when(i + depth - 1 < tiles)
        def _():
            fetch(i + depth - 1).start()

        if not side:

            @pl.when(i == tiles - depth)
            def _():
                hcopy.start()

        at = pl.ds(pl.multiple_of(i * tile, tile), tile)
        part = lax.dot_general(
            gy[...], buf[lax.rem(i, depth)], NT, preferred_element_type=jnp.float32
        )
        if side:
            part += before[:, at]
        o_ref[:, at] = part.astype(o_ref.dtype)

    if not side:
        hcopy.wait()


def down(step, side, pieces, before, wd, hidden):
    half = len(pieces)
    rows, chunk = pieces[0].shape
    width = wd.shape[0]
    span = half * chunk
    tile, depth = 512, 3
    out = [jax.ShapeDtypeStruct((rows, width), jnp.bfloat16 if side else jnp.float32)]
    if not side:
        out.append(jax.ShapeDtypeStruct((2, rows, width), hidden.dtype))
    return pl.pallas_call(
        functools.partial(down_kernel, step, side, tile, half),
        in_specs=[VMEM] * (half + len(before)) + [HBM, HBM],
        out_specs=[VMEM] * len(out),
        out_shape=out,
        scratch_shapes=[
            pltpu.VMEM((depth, tile, span), wd.dtype),
            pltpu.VMEM((rows, span), jnp.bfloat16),
            pltpu.SemaphoreType.DMA((1,)),
            pltpu.SemaphoreType.DMA((depth,)),
        ],
        compiler_params=pltpu.CompilerParams(vmem_limit_bytes=16 << 20),
        cost_estimate=pl.CostEstimate(
            flops=8 * rows * width * span, bytes_accessed=2 * width * span, transcendentals=0
        ),
    )(*pieces, *before, in_hbm(wd), in_hbm(hidden))


def up_tiles(step, dests, tile, gate, upper, wg_ref, wu_ref, x_ref, o_ref, i_ref, bufs, between):
    gbuf, ubuf, xbuf, sem = bufs
    depth = gbuf.shape[0]
    chunk = o_ref.shape[2]
    parts = chunk // tile
    tiles = len(dests) * parts
    col = lax.axis_index("col")
    micro = micro_of(step, x_ref.shape[0])

    def fetch(i):
        k = lax.div(i, parts)
        j = dests[0]
        for at, other in enumerate(dests[1:]):
            j = jnp.where(k == at + 1, other, j)
        dest = lax.bitwise_xor(col, j)
        first = pl.multiple_of(dest * chunk + lax.rem(i, parts) * tile, tile)
        s = lax.rem(i, depth)
        return (
            pltpu.make_async_copy(wg_ref.at[pl.ds(first, tile)], gbuf.at[s], sem.at[0, s]),
            pltpu.make_async_copy(wu_ref.at[pl.ds(first, tile)], ubuf.at[s], sem.at[1, s]),
            pltpu.make_async_copy(x_ref.at[micro, :, pl.ds(first, tile)], xbuf.at[s], sem.at[2, s]),
        )

    def start(i):
        for c in fetch(jnp.int32(i)):
            c.start()

    for i in range(min(depth - 1, tiles)):
        start(i)
    between()
    i_ref[...] = jnp.zeros_like(i_ref)

    @pl.loop(0, tiles)
    def _(i):
        for c in fetch(i):
            c.wait()

        @pl.when(i + depth - 1 < tiles)
        def _():
            start(i + depth - 1)

        s = lax.rem(i, depth)
        acc = lax.dot_general(gate[...], gbuf[s], NT, preferred_element_type=jnp.float32)
        acc += lax.dot_general(upper[...], ubuf[s], NT, preferred_element_type=jnp.float32)
        at = pl.ds(pl.multiple_of(lax.rem(i, parts) * tile, tile), tile)
        o_ref[lax.div(i, parts), :, at] = acc.astype(o_ref.dtype)
        prod = acc * xbuf[s].astype(jnp.float32)
        lanes = i_ref.shape[1]
        total = i_ref[...]
        for b in range(tile // lanes):
            total += prod[:, b * lanes : (b + 1) * lanes]
        i_ref[...] = total


def far_kernel(step, dests, tile, ga, gb, h_ref, wg_ref, wu_ref, x_ref, o_ref, i_ref, gate, upper, *bufs):
    def gradients():
        block = 512

        @pl.loop(0, gate.shape[1] // block)
        def _(b):
            at = pl.ds(pl.multiple_of(b * block, block), block)
            g = ga[:, at].astype(jnp.float32) + gb[:, at].astype(jnp.float32)
            hg = h_ref[0, :, at].astype(jnp.float32)
            hu = h_ref[1, :, at].astype(jnp.float32)
            sig = jax.nn.sigmoid(hg)
            gate[:, at] = (g * hu * sig * (1.0 + hg * (1.0 - sig))).astype(jnp.bfloat16)
            upper[:, at] = (g * hg * sig).astype(jnp.bfloat16)

    up_tiles(step, dests, tile, gate, upper, wg_ref, wu_ref, x_ref, o_ref, i_ref, bufs, gradients)


def near_kernel(step, dests, tile, gate, upper, wg_ref, wu_ref, x_ref, o_ref, i_ref, *bufs):
    up_tiles(step, dests, tile, gate, upper, wg_ref, wu_ref, x_ref, o_ref, i_ref, bufs, lambda: None)


def up_call(kernel, step, dests, operands, wg, wu, inputs, extra):
    feats, width = wg.shape
    rows, chunk = inputs.shape[1], feats // lax.axis_size("col")
    tile, depth = 256, 3
    return pl.pallas_call(
        functools.partial(kernel, step, dests, tile),
        in_specs=[VMEM] * len(operands) + [HBM, HBM, HBM],
        out_specs=[VMEM] * (2 + extra),
        out_shape=[
            jax.ShapeDtypeStruct((len(dests), rows, chunk), jnp.bfloat16),
            jax.ShapeDtypeStruct((rows, 128), jnp.float32),
        ]
        + [jax.ShapeDtypeStruct((rows, width), jnp.bfloat16)] * extra,
        scratch_shapes=[
            pltpu.VMEM((depth, tile, width), wg.dtype),
            pltpu.VMEM((depth, tile, width), wu.dtype),
            pltpu.VMEM((depth, rows, tile), inputs.dtype),
            pltpu.SemaphoreType.DMA((3, depth)),
        ],
        compiler_params=pltpu.CompilerParams(vmem_limit_bytes=24 << 20),
        cost_estimate=pl.CostEstimate(
            flops=16 * rows * width * chunk * len(dests),
            bytes_accessed=4 * width * chunk * len(dests),
            transcendentals=0,
        ),
    )(*operands, in_hbm(wg), in_hbm(wu), in_hbm(inputs))


def shards(cotangent, incoming, upd_u, upd_v, saved_x, saved_h, norm_gain, w_gate, w_up, w_down):
    sections, cols = lax.axis_size("section"), lax.axis_size("col")
    section_idx = lax.axis_index("section")
    inputs_all = saved_x[0].astype(jnp.float32)
    gain = norm_gain[0]
    wg, wu, wd = w_gate[0], w_up[0], w_down[0]
    weighted = (gain * inputs_all).astype(jnp.bfloat16)
    weighted = lax.all_gather(weighted, "col", axis=2, tiled=True)
    sumsq_all = jnp.sum(inputs_all * inputs_all, axis=2)
    rstd_all = None
    half = cols // 2
    far = tuple(range(cols - 1, half - 1, -1))
    near = tuple(range(half - 1, -1, -1))

    carry = cotangent[0]
    for step in range(2 * sections - 1):
        gy = carry.astype(jnp.bfloat16)
        far_pieces = [spread(gy, j) for j in range(half, cols)]
        near_pieces = [spread(gy, j) for j in range(half)]
        carry = rotate(carry)
        micro = (section_idx + step + 1) % sections
        ga, hpair = down(step, 0, near_pieces, [], wd, saved_h)
        (ga,) = down(step, 1, far_pieces, [ga], wd, saved_h)
        gb = swapped(ga, "row", 1)
        outs_far, inner_far, gate, upper = up_call(
            far_kernel, step, far, (ga, gb, hpair), wg, wu, weighted, 2
        )
        normgrad = [swapped(outs_far[k], "col", j) for k, j in enumerate(far)]
        outs_near, inner_near = up_call(near_kernel, step, near, (gate, upper), wg, wu, weighted, 0)
        normgrad += [
            swapped(outs_near[k], "col", j) if j else outs_near[k] for k, j in enumerate(near)
        ]
        inner = jnp.sum(inner_far + inner_near, axis=1)[None]
        if step == 0:
            sums = group_sum(jnp.concatenate([inner, sumsq_all], axis=0))
            inner, rstd_all = sums[:1], lax.rsqrt(sums[1:] / D + eps)
        else:
            inner = group_sum(inner)
        inner = inner[0][:, None] / D
        normgrad = sum(p.astype(jnp.float32) for p in normgrad)
        xf = lax.dynamic_index_in_dim(saved_x[0], micro, 0, keepdims=False).astype(jnp.float32)
        rstd = lax.dynamic_index_in_dim(rstd_all, micro, 0, keepdims=False)[:, None]
        updated = carry + rstd * (gain * normgrad) - xf * (rstd * rstd * rstd) * inner
        active = jnp.logical_and(step >= micro, step - micro < sections)
        carry = jnp.where(active, updated, carry)

    pulled = rotate(carry)
    resid = pulled + incoming[0] - cotangent[0]
    local_dots = jnp.einsum("urd,rd->u", upd_v[0], resid, precision=lax.Precision.HIGHEST)
    dots = group_sum(local_dots)
    update = jnp.einsum("u,urd->rd", dots, upd_u[0], precision=lax.Precision.HIGHEST)
    fresh = cotangent[0] + resid - update
    return (fresh[None], resid[None])


def plain_shards(cotangent, incoming, upd_u, upd_v, saved_x, saved_h, norm_gain, w_gate, w_up, w_down):
    sections = lax.axis_size("section")
    section_idx = lax.axis_index("section")
    inputs_all = saved_x[0].astype(jnp.float32)
    hidden_all = saved_h[0]
    gain = norm_gain[0]
    wg = w_gate[0]
    wu = w_up[0]
    wd = w_down[0]

    def layer_step(step, carry):
        carry = rotate(carry)
        micro = (section_idx + step + 1) % sections
        xf = lax.dynamic_index_in_dim(inputs_all, micro, 0, keepdims=False)
        hpair = lax.dynamic_index_in_dim(hidden_all, micro, 0, keepdims=False)
        sumsq = lax.psum(jnp.sum(xf * xf, axis=1), ("row", "col"))
        gy = carry.astype(jnp.bfloat16)
        wide = lax.all_gather(gy, "col", axis=1, tiled=True)
        ga_part = lax.dot_general(wide, wd, NT, preferred_element_type=jnp.float32)
        ga = lax.psum_scatter(ga_part, "row", scatter_dimension=1, tiled=True)
        width = ga.shape[1]
        offset = lax.axis_index("row") * width
        hg = lax.dynamic_slice_in_dim(hpair[0], offset, width, 1).astype(jnp.float32)
        hu = lax.dynamic_slice_in_dim(hpair[1], offset, width, 1).astype(jnp.float32)
        sig = jax.nn.sigmoid(hg)
        part_gate = (ga * hu * sig * (1.0 + hg * (1.0 - sig))).astype(jnp.bfloat16)
        part_up = (ga * hg * sig).astype(jnp.bfloat16)
        grad_gate = lax.all_gather(part_gate, "row", axis=1, tiled=True)
        grad_up = lax.all_gather(part_up, "row", axis=1, tiled=True)
        first = lax.dot_general(wg, grad_gate, NT, preferred_element_type=jnp.float32)
        second = lax.dot_general(wu, grad_up, NT, preferred_element_type=jnp.float32)
        normgrad = lax.psum_scatter(first + second, "col", scatter_dimension=0, tiled=True).T
        rstd = lax.rsqrt(sumsq / D + eps)[:, None]
        scaled = gain * normgrad
        inner = lax.psum(jnp.sum(scaled * xf, axis=1), ("row", "col"))[:, None] / D
        updated = carry + rstd * scaled - xf * (rstd * rstd * rstd) * inner
        active = jnp.logical_and(step >= micro, step - micro < sections)
        return jnp.where(active, updated, carry)

    pulled = lax.fori_loop(0, 2 * sections - 1, layer_step, cotangent[0])
    pulled = rotate(pulled)
    resid = pulled + incoming[0] - cotangent[0]
    local_dots = jnp.einsum("urd,rd->u", upd_v[0], resid, precision=lax.Precision.HIGHEST)
    dots = lax.psum(local_dots, ("row", "col"))
    update = jnp.einsum("u,urd->rd", dots, upd_u[0], precision=lax.Precision.HIGHEST)
    fresh = cotangent[0] + resid - update
    return (fresh[None], resid[None])


def solution(mesh):
    placed = (
        P("section", None, ("row", "col")),
        P("section", None, ("row", "col")),
        P("section", None, None, ("row", "col")),
        P("section", None, None, ("row", "col")),
        P("section", None, None, ("row", "col")),
        P("section", None, None, None, "col"),
        P("section", ("row", "col")),
        P("section", "row", "col"),
        P("section", "row", "col"),
        P("section", "col", "row"),
    )

    sizes = dict(mesh.shape)
    rows, cols = sizes["row"], sizes["col"]

    def run(*args):
        chunk, width = args[0].shape[2] // (rows * cols), args[7].shape[2] // cols
        paired = rows == 2 and cols > 1 and cols & (cols - 1) == 0
        tuned = paired and chunk % 256 == 0 and width % 512 == 0
        step = jax.shard_map(
            shards if tuned else plain_shards,
            mesh=mesh,
            in_specs=placed,
            out_specs=(P("section", None, ("row", "col")), P("section", None, ("row", "col"))),
            check_vma=False,
        )
        return step(*args)

    return run
```

```python
import functools

import jax
import jax.numpy as jnp
from jax import lax
from jax.experimental import pallas as pl
from jax.experimental.pallas import tpu as pltpu
from jax.sharding import PartitionSpec as P


D = 4096


eps = 1e-05

NT = (((1,), (1,)), ((), ()))
VMEM = pl.BlockSpec(memory_space=pltpu.VMEM)
HBM = pl.BlockSpec(memory_space=pltpu.HBM)


def in_hbm(x):
    return pltpu.with_memory_space_constraint(x, pltpu.HBM)


def shifted(x, axis, by):
    devices = lax.axis_size(axis)
    return lax.ppermute(x, axis, [(i, (i + by) % devices) for i in range(devices)])


def rotate(carry):
    return shifted(carry, "section", -1)


def swapped(x, axis, by):
    return lax.ppermute(x, axis, [(i, i ^ by) for i in range(lax.axis_size(axis))])


def spread(x, by):
    sections, cols = lax.axis_size("section"), lax.axis_size("col")
    pairs = [
        (s * cols + c, ((s - 1) % sections) * cols + (c ^ by))
        for s in range(sections)
        for c in range(cols)
    ]
    return lax.ppermute(x, ("section", "col"), pairs)


def group_sum(x):
    for axis in ("row", "col"):
        by = 1
        while by < lax.axis_size(axis):
            x = x + swapped(x, axis, by)
            by *= 2
    return x


def micro_of(step, sections):
    return lax.rem(lax.axis_index("section") + step + 1, sections)


def bring_kernel(step, cols, ahead, *refs):
    w_ref, sources = refs[0], refs[1 : 1 + ahead]
    other, outs, sem = refs[1 + ahead], refs[2 + ahead : 2 + 2 * ahead], refs[2 + 2 * ahead]
    width, span = other.shape
    group = lax.div(lax.axis_index("col"), cols // 2)
    columns = pl.ds(pl.multiple_of((1 - group) * span, span), span)
    parts = sem.shape[0] - ahead
    copies = []
    for k in range(ahead):
        micro = micro_of(step, sources[k].shape[0])
        copies.append(pltpu.make_async_copy(sources[k].at[micro], outs[k], sem.at[parts + k]))
    for p in range(parts):
        at = pl.ds(p * (width // parts), width // parts)
        copies.append(pltpu.make_async_copy(w_ref.at[at, columns], other.at[at], sem.at[p]))
    for c in copies:
        c.start()
    for c in copies:
        c.wait()


def bring(step, wd, ahead):
    width, span = wd.shape[0], wd.shape[1] // 2
    parts = 4
    size = 2 * width * span
    return pl.pallas_call(
        functools.partial(bring_kernel, step, lax.axis_size("col"), len(ahead)),
        in_specs=[HBM] * (1 + len(ahead)),
        out_specs=[VMEM] * (1 + len(ahead)),
        out_shape=[jax.ShapeDtypeStruct((width, span), wd.dtype)]
        + [jax.ShapeDtypeStruct(x.shape[1:], x.dtype) for x in ahead],
        scratch_shapes=[pltpu.SemaphoreType.DMA((parts + len(ahead),))],
        compiler_params=pltpu.CompilerParams(vmem_limit_bytes=16 << 20),
        cost_estimate=pl.CostEstimate(flops=0, bytes_accessed=size, transcendentals=0),
    )(in_hbm(wd), *[in_hbm(x) for x in ahead])


def near_down_kernel(tile, half, *refs):
    pieces, (w_ref, o_ref, buf, gy, sem) = refs[:half], refs[half:]
    depth, _, span = buf.shape
    tiles = w_ref.shape[0] // tile
    chunk = span // half
    col = lax.axis_index("col")
    group = lax.div(col, half)
    columns = pl.ds(pl.multiple_of(group * span, span), span)

    def fetch(i):
        s = lax.rem(i, depth)
        first = pl.multiple_of(i * tile, tile)
        return pltpu.make_async_copy(w_ref.at[pl.ds(first, tile), columns], buf.at[s], sem.at[s])

    for i in range(depth - 1):
        fetch(i).start()
    for j in range(half):
        source = lax.bitwise_xor(lax.rem(col, half), j)
        gy[:, pl.ds(pl.multiple_of(source * chunk, chunk), chunk)] = pieces[j][...]

    @pl.loop(0, tiles)
    def _(i):
        fetch(i).wait()

        @pl.when(i + depth - 1 < tiles)
        def _():
            fetch(i + depth - 1).start()

        at = pl.ds(pl.multiple_of(i * tile, tile), tile)
        o_ref[:, at] = lax.dot_general(
            gy[...], buf[lax.rem(i, depth)], NT, preferred_element_type=jnp.float32
        )


def near_down(pieces, wd):
    half = len(pieces)
    rows, chunk = pieces[0].shape
    width = wd.shape[0]
    span = half * chunk
    tile, depth = 512, 3
    return pl.pallas_call(
        functools.partial(near_down_kernel, tile, half),
        in_specs=[VMEM] * half + [HBM],
        out_specs=VMEM,
        out_shape=jax.ShapeDtypeStruct((rows, width), jnp.float32),
        scratch_shapes=[
            pltpu.VMEM((depth, tile, span), wd.dtype),
            pltpu.VMEM((rows, span), jnp.bfloat16),
            pltpu.SemaphoreType.DMA((depth,)),
        ],
        compiler_params=pltpu.CompilerParams(vmem_limit_bytes=16 << 20),
        cost_estimate=pl.CostEstimate(
            flops=8 * rows * width * span, bytes_accessed=2 * width * span, transcendentals=0
        ),
    )(*pieces, in_hbm(wd))


def first_tile(far, wg_ref, wu_ref, g_ref, u_ref, sem):
    tile = g_ref.shape[0]
    chunk = wg_ref.shape[0] // lax.axis_size("col")
    dest = lax.bitwise_xor(lax.axis_index("col"), far)
    at = pl.ds(pl.multiple_of(dest * chunk, tile), tile)
    return (
        pltpu.make_async_copy(wg_ref.at[at], g_ref, sem.at[0]),
        pltpu.make_async_copy(wu_ref.at[at], u_ref, sem.at[1]),
    )


def far_down_kernel(tile, half, far, *refs):
    pieces, (before, w_ref, wg_ref, wu_ref, o_ref, g_ref, u_ref, gy, sem) = refs[:half], refs[half:]
    width, span = w_ref.shape
    chunk = span // half
    copies = first_tile(far, wg_ref, wu_ref, g_ref, u_ref, sem)
    for c in copies:
        c.start()
    col = lax.axis_index("col")
    for j in range(half):
        source = lax.bitwise_xor(lax.rem(col, half), j)
        gy[:, pl.ds(pl.multiple_of(source * chunk, chunk), chunk)] = pieces[j][...]

    @pl.loop(0, width // tile)
    def _(i):
        at = pl.ds(pl.multiple_of(i * tile, tile), tile)
        part = before[:, at] + lax.dot_general(
            gy[...], w_ref[at, :], NT, preferred_element_type=jnp.float32
        )
        o_ref[:, at] = part.astype(o_ref.dtype)

    for c in copies:
        c.wait()


TILE = 256


def far_down(pieces, before, weights, wg, wu, far):
    half = len(pieces)
    rows = pieces[0].shape[0]
    width, span = weights.shape
    return pl.pallas_call(
        functools.partial(far_down_kernel, 512, half, far),
        in_specs=[VMEM] * (half + 2) + [HBM, HBM],
        out_specs=[VMEM] * 3,
        out_shape=[jax.ShapeDtypeStruct((rows, width), jnp.bfloat16)]
        + [jax.ShapeDtypeStruct((TILE, width), wg.dtype)] * 2,
        scratch_shapes=[pltpu.VMEM((rows, span), jnp.bfloat16), pltpu.SemaphoreType.DMA((2,))],
        compiler_params=pltpu.CompilerParams(vmem_limit_bytes=16 << 20),
        cost_estimate=pl.CostEstimate(
            flops=8 * rows * width * span, bytes_accessed=2 * width * span, transcendentals=0
        ),
    )(*pieces, before, weights, in_hbm(wg), in_hbm(wu))


def up_tiles(dests, gate, upper, g_ref, u_ref, x_ref, wg_ref, wu_ref, outs, i_ref, after, bufs, between):
    gbuf, ubuf, sem, nsem = bufs
    tile = gbuf.shape[1]
    depth = gbuf.shape[0]
    chunk = outs[0].shape[1]
    parts = chunk // tile
    tiles = len(dests) * parts
    col = lax.axis_index("col")

    def row(i):
        k = lax.div(i, parts)
        j = dests[0]
        for at, other in enumerate(dests[1:]):
            j = jnp.where(k == at + 1, other, j)
        dest = lax.bitwise_xor(col, j)
        return pl.multiple_of(dest * chunk + lax.rem(i, parts) * tile, tile)

    def fetch(i):
        at = pl.ds(row(i), tile)
        s = lax.rem(i, depth)
        return (
            pltpu.make_async_copy(wg_ref.at[at], gbuf.at[s], sem.at[0, s]),
            pltpu.make_async_copy(wu_ref.at[at], ubuf.at[s], sem.at[1, s]),
        )

    def product(i, g, u):
        acc = lax.dot_general(gate[...], g, NT, preferred_element_type=jnp.float32)
        acc += lax.dot_general(upper[...], u, NT, preferred_element_type=jnp.float32)
        if x_ref is not None:
            prod = acc * x_ref[:, pl.ds(row(i), tile)].astype(jnp.float32)
            lanes = i_ref.shape[1]
            total = i_ref[...]
            for b in range(tile // lanes):
                total += prod[:, b * lanes : (b + 1) * lanes]
            i_ref[...] = total
        return acc

    for i in range(1, min(depth, tiles)):
        for c in fetch(jnp.int32(i)):
            c.start()
    between()
    if x_ref is not None:
        i_ref[...] = jnp.zeros_like(i_ref)
    outs[0][:, :tile] = product(jnp.int32(0), g_ref[...], u_ref[...]).astype(outs[0].dtype)

    @pl.loop(1, tiles)
    def _(i):
        for c in fetch(i):
            c.wait()

        @pl.when(i + depth - 1 < tiles)
        def _():
            for c in fetch(i + depth - 1):
                c.start()

        if after is not None:

            @pl.when(i == tiles - 2)
            def _():
                for c in first_tile(*after, nsem):
                    c.start()

        s = lax.rem(i, depth)
        acc = product(i, gbuf[s], ubuf[s])
        at = pl.ds(pl.multiple_of(lax.rem(i, parts) * tile, tile), tile)
        for k in range(len(dests)):

            @pl.when(lax.div(i, parts) == k)
            def _():
                outs[k][:, at] = acc.astype(outs[k].dtype)

    if after is not None:
        for c in first_tile(*after, nsem):
            c.wait()


def far_up_kernel(summed, dests, near, ga, gb, h_ref, g_ref, u_ref, *refs):
    x_ref, refs = (refs[0], refs[1:]) if summed else (None, refs)
    wg_ref, wu_ref, gate, upper, ng_ref, nu_ref, *refs = refs
    i_ref, refs = (refs[0], refs[1:]) if summed else (None, refs)
    outs, bufs = refs[: len(dests)], refs[len(dests) :]

    def gradients():
        block = 512

        @pl.loop(0, gate.shape[1] // block)
        def _(b):
            at = pl.ds(pl.multiple_of(b * block, block), block)
            g = ga[:, at].astype(jnp.float32) + gb[:, at].astype(jnp.float32)
            hg = h_ref[0, :, at].astype(jnp.float32)
            hu = h_ref[1, :, at].astype(jnp.float32)
            sig = jax.nn.sigmoid(hg)
            gate[:, at] = (g * hu * sig * (1.0 + hg * (1.0 - sig))).astype(jnp.bfloat16)
            upper[:, at] = (g * hg * sig).astype(jnp.bfloat16)

    after = (near, wg_ref, wu_ref, ng_ref, nu_ref)
    up_tiles(dests, gate, upper, g_ref, u_ref, x_ref, wg_ref, wu_ref, outs, i_ref, after, bufs, gradients)


def near_up_kernel(summed, dests, near, gate, upper, g_ref, u_ref, *refs):
    x_ref, refs = (refs[0], refs[1:]) if summed else (None, refs)
    wg_ref, wu_ref, *refs = refs
    i_ref, refs = (refs[0], refs[1:]) if summed else (None, refs)
    outs, bufs = refs[: len(dests)], refs[len(dests) :]
    up_tiles(dests, gate, upper, g_ref, u_ref, x_ref, wg_ref, wu_ref, outs, i_ref, None, bufs, lambda: None)


def up_call(kernel, summed, dests, near, operands, wg, wu, extra):
    feats, width = wg.shape
    rows, chunk = operands[0].shape[0], feats // lax.axis_size("col")
    depth = 3
    shapes = [jax.ShapeDtypeStruct(x.shape, x.dtype) for x in extra]
    if summed:
        shapes.append(jax.ShapeDtypeStruct((rows, 128), jnp.float32))
    shapes += [jax.ShapeDtypeStruct((rows, chunk), jnp.bfloat16)] * len(dests)
    return pl.pallas_call(
        functools.partial(kernel, summed, dests, near),
        in_specs=[VMEM] * len(operands) + [HBM, HBM],
        out_specs=[VMEM] * len(shapes),
        out_shape=shapes,
        scratch_shapes=[
            pltpu.VMEM((depth, TILE, width), wg.dtype),
            pltpu.VMEM((depth, TILE, width), wu.dtype),
            pltpu.SemaphoreType.DMA((2, depth)),
            pltpu.SemaphoreType.DMA((2,)),
        ],
        compiler_params=pltpu.CompilerParams(vmem_limit_bytes=28 << 20),
        cost_estimate=pl.CostEstimate(
            flops=16 * rows * width * chunk * len(dests),
            bytes_accessed=4 * width * chunk * len(dests),
            transcendentals=0,
        ),
    )(*operands, in_hbm(wg), in_hbm(wu))


def shards(cotangent, incoming, upd_u, upd_v, saved_x, saved_h, norm_gain, w_gate, w_up, w_down):
    sections, cols = lax.axis_size("section"), lax.axis_size("col")
    section_idx = lax.axis_index("section")
    inputs_all = saved_x[0].astype(jnp.float32)
    gain = norm_gain[0]
    wg, wu, wd = w_gate[0], w_up[0], w_down[0]
    weighted = (gain * inputs_all).astype(jnp.bfloat16)
    weighted = lax.all_gather(weighted, "col", axis=2, tiled=True)
    sumsq_all = jnp.sum(inputs_all * inputs_all, axis=2)
    rstd_all = None
    half = cols // 2
    far = tuple(range(cols - 1, half - 1, -1))
    near = tuple(range(half - 1, -1, -1))

    carry = cotangent[0]
    for step in range(2 * sections - 1):
        gy = carry.astype(jnp.bfloat16)
        near_pieces = [spread(gy, j) for j in range(half)]
        far_pieces = [spread(gy, j) for j in range(half, cols)]
        carry = rotate(carry)
        micro = (section_idx + step + 1) % sections
        summed = step > 0
        ahead = [saved_h[0], weighted] if summed else [saved_h[0]]
        other, hpair, *xs = bring(step, wd, ahead)
        part = near_down(near_pieces, wd)
        ga, *firsts = far_down(far_pieces, part, other, wg, wu, far[0])
        gb = swapped(ga, "row", 1)
        gate, upper, ng, nu, *outs = up_call(
            far_up_kernel, summed, far, near[0], (ga, gb, hpair, *firsts, *xs), wg, wu, [ga, ga, *firsts]
        )
        inner_far, outs_far = outs[: -len(far)], outs[-len(far) :]
        normgrad = [swapped(outs_far[k], "col", j) for k, j in enumerate(far)]
        outs = up_call(near_up_kernel, summed, near, None, (gate, upper, ng, nu, *xs), wg, wu, [])
        inner_near, outs_near = outs[: -len(near)], outs[-len(near) :]
        normgrad += [
            swapped(outs_near[k], "col", j) if j else outs_near[k] for k, j in enumerate(near)
        ]
        xf = lax.dynamic_index_in_dim(saved_x[0], micro, 0, keepdims=False).astype(jnp.float32)
        if summed:
            inner = jnp.sum(inner_far[0] + inner_near[0], axis=1)[None]
            inner = group_sum(inner)
            normgrad = sum(p.astype(jnp.float32) for p in normgrad)
        else:
            normgrad = sum(p.astype(jnp.float32) for p in normgrad)
            inner = jnp.sum(gain * normgrad * xf, axis=1)[None]
            sums = group_sum(jnp.concatenate([inner, sumsq_all], axis=0))
            inner, rstd_all = sums[:1], lax.rsqrt(sums[1:] / D + eps)
        inner = inner[0][:, None] / D
        rstd = lax.dynamic_index_in_dim(rstd_all, micro, 0, keepdims=False)[:, None]
        updated = carry + rstd * (gain * normgrad) - xf * (rstd * rstd * rstd) * inner
        active = jnp.logical_and(step >= micro, step - micro < sections)
        carry = jnp.where(active, updated, carry)

    pulled = rotate(carry)
    resid = pulled + incoming[0] - cotangent[0]
    local_dots = jnp.sum(upd_v[0] * resid[None], axis=(1, 2))
    dots = group_sum(local_dots)
    update = jnp.sum(dots[:, None, None] * upd_u[0], axis=0)
    fresh = cotangent[0] + resid - update
    return (fresh[None], resid[None])


def plain_shards(cotangent, incoming, upd_u, upd_v, saved_x, saved_h, norm_gain, w_gate, w_up, w_down):
    sections = lax.axis_size("section")
    section_idx = lax.axis_index("section")
    inputs_all = saved_x[0].astype(jnp.float32)
    hidden_all = saved_h[0]
    gain = norm_gain[0]
    wg = w_gate[0]
    wu = w_up[0]
    wd = w_down[0]

    def layer_step(step, carry):
        carry = rotate(carry)
        micro = (section_idx + step + 1) % sections
        xf = lax.dynamic_index_in_dim(inputs_all, micro, 0, keepdims=False)
        hpair = lax.dynamic_index_in_dim(hidden_all, micro, 0, keepdims=False)
        sumsq = lax.psum(jnp.sum(xf * xf, axis=1), ("row", "col"))
        gy = carry.astype(jnp.bfloat16)
        wide = lax.all_gather(gy, "col", axis=1, tiled=True)
        ga_part = lax.dot_general(wide, wd, NT, preferred_element_type=jnp.float32)
        ga = lax.psum_scatter(ga_part, "row", scatter_dimension=1, tiled=True)
        width = ga.shape[1]
        offset = lax.axis_index("row") * width
        hg = lax.dynamic_slice_in_dim(hpair[0], offset, width, 1).astype(jnp.float32)
        hu = lax.dynamic_slice_in_dim(hpair[1], offset, width, 1).astype(jnp.float32)
        sig = jax.nn.sigmoid(hg)
        part_gate = (ga * hu * sig * (1.0 + hg * (1.0 - sig))).astype(jnp.bfloat16)
        part_up = (ga * hg * sig).astype(jnp.bfloat16)
        grad_gate = lax.all_gather(part_gate, "row", axis=1, tiled=True)
        grad_up = lax.all_gather(part_up, "row", axis=1, tiled=True)
        first = lax.dot_general(wg, grad_gate, NT, preferred_element_type=jnp.float32)
        second = lax.dot_general(wu, grad_up, NT, preferred_element_type=jnp.float32)
        normgrad = lax.psum_scatter(first + second, "col", scatter_dimension=0, tiled=True).T
        rstd = lax.rsqrt(sumsq / D + eps)[:, None]
        scaled = gain * normgrad
        inner = lax.psum(jnp.sum(scaled * xf, axis=1), ("row", "col"))[:, None] / D
        updated = carry + rstd * scaled - xf * (rstd * rstd * rstd) * inner
        active = jnp.logical_and(step >= micro, step - micro < sections)
        return jnp.where(active, updated, carry)

    pulled = lax.fori_loop(0, 2 * sections - 1, layer_step, cotangent[0])
    pulled = rotate(pulled)
    resid = pulled + incoming[0] - cotangent[0]
    local_dots = jnp.einsum("urd,rd->u", upd_v[0], resid, precision=lax.Precision.HIGHEST)
    dots = lax.psum(local_dots, ("row", "col"))
    update = jnp.einsum("u,urd->rd", dots, upd_u[0], precision=lax.Precision.HIGHEST)
    fresh = cotangent[0] + resid - update
    return (fresh[None], resid[None])


def solution(mesh):
    placed = (
        P("section", None, ("row", "col")),
        P("section", None, ("row", "col")),
        P("section", None, None, ("row", "col")),
        P("section", None, None, ("row", "col")),
        P("section", None, None, ("row", "col")),
        P("section", None, None, None, "col"),
        P("section", ("row", "col")),
        P("section", "row", "col"),
        P("section", "row", "col"),
        P("section", "col", "row"),
    )

    sizes = dict(mesh.shape)
    rows, cols = sizes["row"], sizes["col"]

    def run(*args):
        chunk, width = args[0].shape[2] // (rows * cols), args[7].shape[2] // cols
        paired = rows == 2 and cols > 1 and cols & (cols - 1) == 0
        tuned = paired and chunk % 256 == 0 and width % 512 == 0
        step = jax.shard_map(
            shards if tuned else plain_shards,
            mesh=mesh,
            in_specs=placed,
            out_specs=(P("section", None, ("row", "col")), P("section", None, ("row", "col"))),
            check_vma=False,
        )
        return step(*args)

    return run
```

```python
import functools

import jax
import jax.numpy as jnp
from jax import lax
from jax.experimental import pallas as pl
from jax.experimental.pallas import tpu as pltpu
from jax.sharding import PartitionSpec as P


D = 4096


eps = 1e-05

NT = (((1,), (1,)), ((), ()))
VMEM = pl.BlockSpec(memory_space=pltpu.VMEM)
HBM = pl.BlockSpec(memory_space=pltpu.HBM)


def in_hbm(x):
    return pltpu.with_memory_space_constraint(x, pltpu.HBM)


def shifted(x, axis, by):
    devices = lax.axis_size(axis)
    return lax.ppermute(x, axis, [(i, (i + by) % devices) for i in range(devices)])


def rotate(carry):
    return shifted(carry, "section", -1)


def swapped(x, axis, by):
    return lax.ppermute(x, axis, [(i, i ^ by) for i in range(lax.axis_size(axis))])


def spread(x, by):
    sections, cols = lax.axis_size("section"), lax.axis_size("col")
    pairs = [
        (s * cols + c, ((s - 1) % sections) * cols + (c ^ by))
        for s in range(sections)
        for c in range(cols)
    ]
    return lax.ppermute(x, ("section", "col"), pairs)


def group_sum(x):
    for axis in ("row", "col"):
        by = 1
        while by < lax.axis_size(axis):
            x = x + swapped(x, axis, by)
            by *= 2
    return x


def micro_of(step, sections):
    return lax.rem(lax.axis_index("section") + step + 1, sections)


def bring_kernel(step, cols, ahead, *refs):
    w_ref, sources = refs[0], refs[1 : 1 + ahead]
    other, outs, sem = refs[1 + ahead], refs[2 + ahead : 2 + 2 * ahead], refs[2 + 2 * ahead]
    width, span = other.shape
    group = lax.div(lax.axis_index("col"), cols // 2)
    columns = pl.ds(pl.multiple_of((1 - group) * span, span), span)
    parts = sem.shape[0] - ahead
    copies = []
    for k in range(ahead):
        micro = micro_of(step, sources[k].shape[0])
        copies.append(pltpu.make_async_copy(sources[k].at[micro], outs[k], sem.at[parts + k]))
    for p in range(parts):
        at = pl.ds(p * (width // parts), width // parts)
        copies.append(pltpu.make_async_copy(w_ref.at[at, columns], other.at[at], sem.at[p]))
    for c in copies:
        c.start()
    for c in copies:
        c.wait()


def bring(step, wd, ahead):
    width, span = wd.shape[0], wd.shape[1] // 2
    parts = 4
    size = 2 * width * span
    return pl.pallas_call(
        functools.partial(bring_kernel, step, lax.axis_size("col"), len(ahead)),
        in_specs=[HBM] * (1 + len(ahead)),
        out_specs=[VMEM] * (1 + len(ahead)),
        out_shape=[jax.ShapeDtypeStruct((width, span), wd.dtype)]
        + [jax.ShapeDtypeStruct(x.shape[1:], x.dtype) for x in ahead],
        scratch_shapes=[pltpu.SemaphoreType.DMA((parts + len(ahead),))],
        compiler_params=pltpu.CompilerParams(vmem_limit_bytes=16 << 20),
        cost_estimate=pl.CostEstimate(flops=0, bytes_accessed=size, transcendentals=0),
    )(in_hbm(wd), *[in_hbm(x) for x in ahead])


def near_down_kernel(tile, half, *refs):
    pieces, (w_ref, o_ref, buf, gy, sem) = refs[:half], refs[half:]
    depth, _, span = buf.shape
    tiles = w_ref.shape[0] // tile
    chunk = span // half
    col = lax.axis_index("col")
    group = lax.div(col, half)
    columns = pl.ds(pl.multiple_of(group * span, span), span)

    def fetch(i):
        s = lax.rem(i, depth)
        first = pl.multiple_of(i * tile, tile)
        return pltpu.make_async_copy(w_ref.at[pl.ds(first, tile), columns], buf.at[s], sem.at[s])

    for i in range(depth - 1):
        fetch(i).start()
    for j in range(half):
        source = lax.bitwise_xor(lax.rem(col, half), j)
        gy[:, pl.ds(pl.multiple_of(source * chunk, chunk), chunk)] = pieces[j][...]

    @pl.loop(0, tiles)
    def _(i):
        fetch(i).wait()

        @pl.when(i + depth - 1 < tiles)
        def _():
            fetch(i + depth - 1).start()

        at = pl.ds(pl.multiple_of(i * tile, tile), tile)
        o_ref[:, at] = lax.dot_general(
            gy[...], buf[lax.rem(i, depth)], NT, preferred_element_type=jnp.float32
        )


def down_tile(width):
    return 896 if width % 896 == 0 else 512


def near_down(pieces, wd):
    half = len(pieces)
    rows, chunk = pieces[0].shape
    width = wd.shape[0]
    span = half * chunk
    tile, depth = down_tile(width), 3
    return pl.pallas_call(
        functools.partial(near_down_kernel, tile, half),
        in_specs=[VMEM] * half + [HBM],
        out_specs=VMEM,
        out_shape=jax.ShapeDtypeStruct((rows, width), jnp.float32),
        scratch_shapes=[
            pltpu.VMEM((depth, tile, span), wd.dtype),
            pltpu.VMEM((rows, span), jnp.bfloat16),
            pltpu.SemaphoreType.DMA((depth,)),
        ],
        compiler_params=pltpu.CompilerParams(vmem_limit_bytes=16 << 20),
        cost_estimate=pl.CostEstimate(
            flops=8 * rows * width * span, bytes_accessed=2 * width * span, transcendentals=0
        ),
    )(*pieces, in_hbm(wd))


def first_tile(far, wg_ref, wu_ref, g_ref, u_ref, sem):
    tile = g_ref.shape[0]
    chunk = wg_ref.shape[0] // lax.axis_size("col")
    dest = lax.bitwise_xor(lax.axis_index("col"), far)
    at = pl.ds(pl.multiple_of(dest * chunk, tile), tile)
    return (
        pltpu.make_async_copy(wg_ref.at[at], g_ref, sem.at[0]),
        pltpu.make_async_copy(wu_ref.at[at], u_ref, sem.at[1]),
    )


def far_down_kernel(tile, half, far, *refs):
    pieces, (before, w_ref, wg_ref, wu_ref, o_ref, g_ref, u_ref, gy, sem) = refs[:half], refs[half:]
    width, span = w_ref.shape
    chunk = span // half
    copies = first_tile(far, wg_ref, wu_ref, g_ref, u_ref, sem)
    for c in copies:
        c.start()
    col = lax.axis_index("col")
    for j in range(half):
        source = lax.bitwise_xor(lax.rem(col, half), j)
        gy[:, pl.ds(pl.multiple_of(source * chunk, chunk), chunk)] = pieces[j][...]

    @pl.loop(0, width // tile)
    def _(i):
        at = pl.ds(pl.multiple_of(i * tile, tile), tile)
        part = before[:, at] + lax.dot_general(
            gy[...], w_ref[at, :], NT, preferred_element_type=jnp.float32
        )
        o_ref[:, at] = part.astype(o_ref.dtype)

    for c in copies:
        c.wait()


TILE = 256


def far_down(pieces, before, weights, wg, wu, far):
    half = len(pieces)
    rows = pieces[0].shape[0]
    width, span = weights.shape
    return pl.pallas_call(
        functools.partial(far_down_kernel, down_tile(width), half, far),
        in_specs=[VMEM] * (half + 2) + [HBM, HBM],
        out_specs=[VMEM] * 3,
        out_shape=[jax.ShapeDtypeStruct((rows, width), jnp.bfloat16)]
        + [jax.ShapeDtypeStruct((TILE, width), wg.dtype)] * 2,
        scratch_shapes=[pltpu.VMEM((rows, span), jnp.bfloat16), pltpu.SemaphoreType.DMA((2,))],
        compiler_params=pltpu.CompilerParams(vmem_limit_bytes=16 << 20),
        cost_estimate=pl.CostEstimate(
            flops=8 * rows * width * span, bytes_accessed=2 * width * span, transcendentals=0
        ),
    )(*pieces, before, weights, in_hbm(wg), in_hbm(wu))


def up_tiles(dests, gate, upper, g_ref, u_ref, x_ref, wg_ref, wu_ref, outs, i_ref, after, bufs, between):
    gbuf, ubuf, sem, nsem = bufs
    tile = gbuf.shape[1]
    depth = gbuf.shape[0]
    chunk = outs[0].shape[1]
    parts = chunk // tile
    tiles = len(dests) * parts
    col = lax.axis_index("col")

    def row(i):
        k = lax.div(i, parts)
        j = dests[0]
        for at, other in enumerate(dests[1:]):
            j = jnp.where(k == at + 1, other, j)
        dest = lax.bitwise_xor(col, j)
        return pl.multiple_of(dest * chunk + lax.rem(i, parts) * tile, tile)

    def fetch(i):
        at = pl.ds(row(i), tile)
        s = lax.rem(i, depth)
        return (
            pltpu.make_async_copy(wg_ref.at[at], gbuf.at[s], sem.at[0, s]),
            pltpu.make_async_copy(wu_ref.at[at], ubuf.at[s], sem.at[1, s]),
        )

    def product(i, g, u):
        acc = lax.dot_general(gate[...], g, NT, preferred_element_type=jnp.float32)
        acc += lax.dot_general(upper[...], u, NT, preferred_element_type=jnp.float32)
        if x_ref is not None:
            prod = acc * x_ref[:, pl.ds(row(i), tile)].astype(jnp.float32)
            lanes = i_ref.shape[1]
            total = i_ref[...]
            for b in range(tile // lanes):
                total += prod[:, b * lanes : (b + 1) * lanes]
            i_ref[...] = total
        return acc

    for i in range(1, min(depth, tiles)):
        for c in fetch(jnp.int32(i)):
            c.start()
    between()
    if x_ref is not None:
        i_ref[...] = jnp.zeros_like(i_ref)
    outs[0][:, :tile] = product(jnp.int32(0), g_ref[...], u_ref[...]).astype(outs[0].dtype)

    @pl.loop(1, tiles)
    def _(i):
        for c in fetch(i):
            c.wait()

        @pl.when(i + depth - 1 < tiles)
        def _():
            for c in fetch(i + depth - 1):
                c.start()

        if after is not None:

            @pl.when(i == tiles - 2)
            def _():
                for c in first_tile(*after, nsem):
                    c.start()

        s = lax.rem(i, depth)
        acc = product(i, gbuf[s], ubuf[s])
        at = pl.ds(pl.multiple_of(lax.rem(i, parts) * tile, tile), tile)
        for k in range(len(dests)):

            @pl.when(lax.div(i, parts) == k)
            def _():
                outs[k][:, at] = acc.astype(outs[k].dtype)

    if after is not None:
        for c in first_tile(*after, nsem):
            c.wait()


def far_up_kernel(summed, dests, near, ga, gb, h_ref, g_ref, u_ref, *refs):
    x_ref, refs = (refs[0], refs[1:]) if summed else (None, refs)
    wg_ref, wu_ref, gate, upper, ng_ref, nu_ref, *refs = refs
    i_ref, refs = (refs[0], refs[1:]) if summed else (None, refs)
    outs, bufs = refs[: len(dests)], refs[len(dests) :]

    def gradients():
        block = 256

        @pl.loop(0, gate.shape[1] // block)
        def _(b):
            at = pl.ds(pl.multiple_of(b * block, block), block)
            g = ga[:, at].astype(jnp.float32) + gb[:, at].astype(jnp.float32)
            hg = h_ref[0, :, at].astype(jnp.float32)
            hu = h_ref[1, :, at].astype(jnp.float32)
            sig = jax.nn.sigmoid(hg)
            gate[:, at] = (g * hu * sig * (1.0 + hg * (1.0 - sig))).astype(jnp.bfloat16)
            upper[:, at] = (g * hg * sig).astype(jnp.bfloat16)

    after = (near, wg_ref, wu_ref, ng_ref, nu_ref)
    up_tiles(dests, gate, upper, g_ref, u_ref, x_ref, wg_ref, wu_ref, outs, i_ref, after, bufs, gradients)


def near_up_kernel(summed, dests, near, gate, upper, g_ref, u_ref, *refs):
    x_ref, refs = (refs[0], refs[1:]) if summed else (None, refs)
    wg_ref, wu_ref, *refs = refs
    i_ref, refs = (refs[0], refs[1:]) if summed else (None, refs)
    outs, bufs = refs[: len(dests)], refs[len(dests) :]
    up_tiles(dests, gate, upper, g_ref, u_ref, x_ref, wg_ref, wu_ref, outs, i_ref, None, bufs, lambda: None)


def up_call(kernel, summed, dests, near, operands, wg, wu, extra):
    feats, width = wg.shape
    rows, chunk = operands[0].shape[0], feats // lax.axis_size("col")
    depth = 3
    shapes = [jax.ShapeDtypeStruct(x.shape, x.dtype) for x in extra]
    if summed:
        shapes.append(jax.ShapeDtypeStruct((rows, 128), jnp.float32))
    shapes += [jax.ShapeDtypeStruct((rows, chunk), jnp.bfloat16)] * len(dests)
    return pl.pallas_call(
        functools.partial(kernel, summed, dests, near),
        in_specs=[VMEM] * len(operands) + [HBM, HBM],
        out_specs=[VMEM] * len(shapes),
        out_shape=shapes,
        scratch_shapes=[
            pltpu.VMEM((depth, TILE, width), wg.dtype),
            pltpu.VMEM((depth, TILE, width), wu.dtype),
            pltpu.SemaphoreType.DMA((2, depth)),
            pltpu.SemaphoreType.DMA((2,)),
        ],
        compiler_params=pltpu.CompilerParams(vmem_limit_bytes=28 << 20),
        cost_estimate=pl.CostEstimate(
            flops=16 * rows * width * chunk * len(dests),
            bytes_accessed=4 * width * chunk * len(dests),
            transcendentals=0,
        ),
    )(*operands, in_hbm(wg), in_hbm(wu))


def shards(cotangent, incoming, upd_u, upd_v, saved_x, saved_h, norm_gain, w_gate, w_up, w_down):
    sections, cols = lax.axis_size("section"), lax.axis_size("col")
    section_idx = lax.axis_index("section")
    inputs_all = saved_x[0].astype(jnp.float32)
    gain = norm_gain[0]
    wg, wu, wd = w_gate[0], w_up[0], w_down[0]
    weighted = (gain * inputs_all).astype(jnp.bfloat16)
    weighted = lax.all_gather(weighted, "col", axis=2, tiled=True)
    sumsq_all = jnp.sum(inputs_all * inputs_all, axis=2)
    rstd_all = None
    half = cols // 2
    far = tuple(range(cols - 1, half - 1, -1))
    near = tuple(range(half - 1, -1, -1))

    carry = cotangent[0]
    for step in range(2 * sections - 1):
        gy = carry.astype(jnp.bfloat16)
        if step == 0:
            gy, sumsq_all = lax.optimization_barrier((gy, sumsq_all))
        near_pieces = [spread(gy, j) for j in range(half)]
        far_pieces = [spread(gy, j) for j in range(half, cols)]
        carry = rotate(carry)
        micro = (section_idx + step + 1) % sections
        summed = step > 0
        ahead = [saved_h[0], weighted] if summed else [saved_h[0]]
        other, hpair, *xs = bring(step, wd, ahead)
        part = near_down(near_pieces, wd)
        ga, *firsts = far_down(far_pieces, part, other, wg, wu, far[0])
        gb = swapped(ga, "row", 1)
        gate, upper, ng, nu, *outs = up_call(
            far_up_kernel, summed, far, near[0], (ga, gb, hpair, *firsts, *xs), wg, wu, [ga, ga, *firsts]
        )
        inner_far, outs_far = outs[: -len(far)], outs[-len(far) :]
        normgrad = [swapped(outs_far[k], "col", j) for k, j in enumerate(far)]
        outs = up_call(near_up_kernel, summed, near, None, (gate, upper, ng, nu, *xs), wg, wu, [])
        inner_near, outs_near = outs[: -len(near)], outs[-len(near) :]
        normgrad += [
            swapped(outs_near[k], "col", j) if j else outs_near[k] for k, j in enumerate(near)
        ]
        xf = lax.dynamic_index_in_dim(saved_x[0], micro, 0, keepdims=False).astype(jnp.float32)
        if summed:
            inner = jnp.sum(inner_far[0] + inner_near[0], axis=1)[None]
            inner = group_sum(inner)
            normgrad = sum(p.astype(jnp.float32) for p in normgrad)
        else:
            normgrad = sum(p.astype(jnp.float32) for p in normgrad)
            inner = jnp.sum(gain * normgrad * xf, axis=1)[None]
            sums = group_sum(jnp.concatenate([inner, sumsq_all], axis=0))
            inner, rstd_all = sums[:1], lax.rsqrt(sums[1:] / D + eps)
        inner = inner[0][:, None] / D
        rstd = lax.dynamic_index_in_dim(rstd_all, micro, 0, keepdims=False)[:, None]
        updated = carry + rstd * (gain * normgrad) - xf * (rstd * rstd * rstd) * inner
        active = jnp.logical_and(step >= micro, step - micro < sections)
        carry = jnp.where(active, updated, carry)

    pulled = rotate(carry)
    resid = pulled + incoming[0] - cotangent[0]
    local_dots = jnp.sum(upd_v[0] * resid[None], axis=(1, 2))
    dots = group_sum(local_dots)
    update = jnp.sum(dots[:, None, None] * upd_u[0], axis=0)
    fresh = cotangent[0] + resid - update
    return (fresh[None], resid[None])


def plain_shards(cotangent, incoming, upd_u, upd_v, saved_x, saved_h, norm_gain, w_gate, w_up, w_down):
    sections = lax.axis_size("section")
    section_idx = lax.axis_index("section")
    inputs_all = saved_x[0].astype(jnp.float32)
    hidden_all = saved_h[0]
    gain = norm_gain[0]
    wg = w_gate[0]
    wu = w_up[0]
    wd = w_down[0]

    def layer_step(step, carry):
        carry = rotate(carry)
        micro = (section_idx + step + 1) % sections
        xf = lax.dynamic_index_in_dim(inputs_all, micro, 0, keepdims=False)
        hpair = lax.dynamic_index_in_dim(hidden_all, micro, 0, keepdims=False)
        sumsq = lax.psum(jnp.sum(xf * xf, axis=1), ("row", "col"))
        gy = carry.astype(jnp.bfloat16)
        wide = lax.all_gather(gy, "col", axis=1, tiled=True)
        ga_part = lax.dot_general(wide, wd, NT, preferred_element_type=jnp.float32)
        ga = lax.psum_scatter(ga_part, "row", scatter_dimension=1, tiled=True)
        width = ga.shape[1]
        offset = lax.axis_index("row") * width
        hg = lax.dynamic_slice_in_dim(hpair[0], offset, width, 1).astype(jnp.float32)
        hu = lax.dynamic_slice_in_dim(hpair[1], offset, width, 1).astype(jnp.float32)
        sig = jax.nn.sigmoid(hg)
        part_gate = (ga * hu * sig * (1.0 + hg * (1.0 - sig))).astype(jnp.bfloat16)
        part_up = (ga * hg * sig).astype(jnp.bfloat16)
        grad_gate = lax.all_gather(part_gate, "row", axis=1, tiled=True)
        grad_up = lax.all_gather(part_up, "row", axis=1, tiled=True)
        first = lax.dot_general(wg, grad_gate, NT, preferred_element_type=jnp.float32)
        second = lax.dot_general(wu, grad_up, NT, preferred_element_type=jnp.float32)
        normgrad = lax.psum_scatter(first + second, "col", scatter_dimension=0, tiled=True).T
        rstd = lax.rsqrt(sumsq / D + eps)[:, None]
        scaled = gain * normgrad
        inner = lax.psum(jnp.sum(scaled * xf, axis=1), ("row", "col"))[:, None] / D
        updated = carry + rstd * scaled - xf * (rstd * rstd * rstd) * inner
        active = jnp.logical_and(step >= micro, step - micro < sections)
        return jnp.where(active, updated, carry)

    pulled = lax.fori_loop(0, 2 * sections - 1, layer_step, cotangent[0])
    pulled = rotate(pulled)
    resid = pulled + incoming[0] - cotangent[0]
    local_dots = jnp.einsum("urd,rd->u", upd_v[0], resid, precision=lax.Precision.HIGHEST)
    dots = lax.psum(local_dots, ("row", "col"))
    update = jnp.einsum("u,urd->rd", dots, upd_u[0], precision=lax.Precision.HIGHEST)
    fresh = cotangent[0] + resid - update
    return (fresh[None], resid[None])


def solution(mesh):
    placed = (
        P("section", None, ("row", "col")),
        P("section", None, ("row", "col")),
        P("section", None, None, ("row", "col")),
        P("section", None, None, ("row", "col")),
        P("section", None, None, ("row", "col")),
        P("section", None, None, None, "col"),
        P("section", ("row", "col")),
        P("section", "row", "col"),
        P("section", "row", "col"),
        P("section", "col", "row"),
    )

    sizes = dict(mesh.shape)
    rows, cols = sizes["row"], sizes["col"]

    def run(*args):
        chunk, width = args[0].shape[2] // (rows * cols), args[7].shape[2] // cols
        paired = rows == 2 and cols > 1 and cols & (cols - 1) == 0
        tuned = paired and chunk % 256 == 0 and width % 512 == 0
        step = jax.shard_map(
            shards if tuned else plain_shards,
            mesh=mesh,
            in_specs=placed,
            out_specs=(P("section", None, ("row", "col")), P("section", None, ("row", "col"))),
            check_vma=False,
        )
        return step(*args)

    return run
```
